32 devices in a mesh: row: 4 (over y, core), col: 8 (over z, x).
Axes of the slice: x: 2, y: 2, z: 4, core: 2. Of those that a mesh axis runs over, the one named last changes fastest.
Arguments:
- calib: bfloat16 [256, 8192], replicated, may hold values from -6 to 6
- gate_a: bfloat16 [8192, 28672], P('col', 'row'), may hold values from -0.0625 to 0.0625
- up_a: bfloat16 [8192, 28672], P('col', 'row'), may hold values from -0.0625 to 0.0625
- gate_b: bfloat16 [8192, 28672], P('row', 'col'), may hold values from -0.0625 to 0.0625
- up_b: bfloat16 [8192, 28672], P('row', 'col'), may hold values from -0.0625 to 0.0625
- down_a: bfloat16 [28672, 1024], P(('row', 'col')), may hold values from -6 to 6
- down_b: bfloat16 [28672, 1024], P('col', 'row'), may hold values from -6 to 6
Outputs:
- joined: bfloat16 [28672, 1024], P(('row', 'col'))
The draws below stay inside these ranges and needn't reach their ends.
All inputs are finite; a program needn't handle non-finite values.
Results may differ from the reference program's by a relative error of at most 0.025.
Values may be sent and summed in bfloat16 or wider, within the bound.
A program may use at most 384 MiB of HBM per device.

```python
import jax
import jax.numpy as jnp
from jax import lax

D = 8192
FF = 28672
CALIB_TOKENS = 256
DW = 1024
ITERS = 3
BLOCK_B = 3584
N_ROW = 4
N_COL = 8


def levels(rng, shape, shards, low, high):
    def one(dim, blocks):
        draws = jax.random.uniform(jax.random.fold_in(jax.random.fold_in(rng, 6), dim), (blocks,), jnp.float32, low / len(shards), high / len(shards))
        return jnp.repeat(jnp.exp(draws), shape[dim] // blocks).reshape((-1,) + (1,) * (len(shape) - dim - 1))

    level = one(*shards[0])
    for cut in shards[1:]:
        level = level * one(*cut)
    return level


def scatter_about(key, extent, deviation, reach, pieces=(), held_as=jnp.bfloat16):
    values = deviation * jax.random.normal(key, extent, jnp.float32)
    if pieces:
        values = values * levels(key, extent, pieces, -0.22, 0.18)
    return jnp.clip(values, -reach, reach).astype(held_as)


def setup_inputs(seed: int = 0) -> dict:
    keys = jax.random.split(jax.random.key(seed), 8)
    return {
        "calib": scatter_about(keys[0], (CALIB_TOKENS, D), 1.0, 6.0),
        "gate_a": scatter_about(keys[1], (D, FF), D ** -0.5, 0.0625, ((0, 8), (1, 4))),
        "up_a": scatter_about(keys[2], (D, FF), D ** -0.5, 0.0625, ((0, 8), (1, 4))),
        "gate_b": scatter_about(keys[3], (D, FF), D ** -0.5, 0.0625, ((0, 4), (1, 8))),
        "up_b": scatter_about(keys[4], (D, FF), D ** -0.5, 0.0625, ((0, 4), (1, 8))),
        "down_a": scatter_about(keys[5], (FF, DW), 1.0, 6.0, ((0, 32),)),
        "down_b": scatter_about(keys[6], (FF, DW), 1.0, 6.0, ((0, 8), (1, 4))),
    }


softness = 0.02
statistic_floor = 1e-05

def standardize(gate_pre, up_preactivation):
    hidden = jax.nn.silu(gate_pre) * up_preactivation
    center = lax.optimization_barrier(jnp.mean(hidden, axis=0, keepdims=True))
    spread = lax.optimization_barrier(jnp.mean(jnp.square(hidden - center), axis=0, keepdims=True))
    return ((hidden - center) * lax.rsqrt(spread + statistic_floor)).astype(jnp.bfloat16)

def reference(calib, gate_a, up_a, gate_b, up_b, down_a, down_b):
    first_model_scores = standardize(jnp.dot(calib, gate_a, preferred_element_type=jnp.float32), jnp.dot(calib, up_a, preferred_element_type=jnp.float32))
    scores_b = standardize(jnp.dot(calib, gate_b, preferred_element_type=jnp.float32), jnp.dot(calib, up_b, preferred_element_type=jnp.float32))
    row_block = FF // N_ROW
    multiplier = 1.0 / (CALIB_TOKENS * softness)

    def kernel_rows(index):
        start = (index * row_block).astype(jnp.int32)
        rows_a = lax.dynamic_slice_in_dim(first_model_scores, start, row_block, 1)
        return jnp.exp(jnp.dot(rows_a.T, scores_b, preferred_element_type=jnp.float32) * multiplier)
    kernel = lax.map(kernel_rows, jnp.arange(N_ROW, dtype=jnp.int32)).reshape(FF, FF)
    column_scaling = jnp.ones((FF,), jnp.float32)
    for step in range(ITERS):
        row_scale = 1.0 / jnp.dot(kernel, column_scaling, precision=lax.Precision.HIGHEST)
        column_scaling = 1.0 / jnp.dot(row_scale, kernel, precision=lax.Precision.HIGHEST)

    def add_block(index, total):
        start = (index * BLOCK_B).astype(jnp.int32)
        kernel_cols = lax.dynamic_slice_in_dim(kernel, start, BLOCK_B, 1)
        scale_cols = lax.dynamic_slice_in_dim(column_scaling, start, BLOCK_B, 0)
        plan = (row_scale[:, None] * kernel_cols * scale_cols[None, :]).astype(jnp.bfloat16)
        rows_b = lax.dynamic_slice_in_dim(down_b, start, BLOCK_B, 0)
        part = jnp.dot(plan, rows_b, preferred_element_type=jnp.float32).astype(jnp.bfloat16)
        part = lax.optimization_barrier(part)
        return total + part.astype(jnp.float32)
    aligned = lax.fori_loop(0, N_COL, add_block, jnp.zeros((FF, DW), jnp.float32))
    return ((down_a.astype(jnp.float32) + aligned) * 0.5).astype(jnp.bfloat16)
```

```python
import jax
import jax.numpy as jnp
from jax import lax
from jax.experimental import pallas as pl
from jax.experimental.pallas import tpu as pltpu
from jax.sharding import PartitionSpec as P

ITERS = 3


softness = 0.02
statistic_floor = 1e-05
LANES = 128


def standardize(gate_pre, up_preactivation):
    hidden = jax.nn.silu(gate_pre) * up_preactivation
    center = jnp.mean(hidden, axis=0, keepdims=True)
    spread = jnp.mean(jnp.square(hidden - center), axis=0, keepdims=True)
    return ((hidden - center) * lax.rsqrt(spread + statistic_floor)).astype(jnp.bfloat16)


def block_of(size, most):
    block = most
    while size % block:
        block //= 2
    return block


def lane_chunk(size, most):
    chunk = most
    while size % chunk:
        chunk -= LANES
    return chunk


def make_kernel(scores_a, scores_b, multiplier):
    rows, depth = scores_a.shape
    cols = scores_b.shape[0]
    block = block_of(rows, 512)
    chunk = lane_chunk(cols, 512)

    def body(a_ref, b_ref, k_ref, s_ref):
        total = jnp.zeros((block, LANES), jnp.float32)
        for start in range(0, cols, chunk):
            logits = lax.dot_general(
                a_ref[...], b_ref[start : start + chunk, :], (((1,), (1,)), ((), ())),
                preferred_element_type=jnp.float32,
            )
            values = jnp.exp(logits * multiplier)
            k_ref[:, start : start + chunk] = values.astype(jnp.bfloat16)
            for lane in range(0, chunk, LANES):
                total = total + values[:, lane : lane + LANES]
        s_ref[...] = jnp.sum(total, axis=1, keepdims=True)

    return pl.pallas_call(
        body,
        grid=(rows // block,),
        in_specs=[
            pl.BlockSpec((block, depth), lambda i: (i, 0)),
            pl.BlockSpec((cols, depth), lambda i: (0, 0)),
        ],
        out_specs=[
            pl.BlockSpec((block, cols), lambda i: (i, 0)),
            pl.BlockSpec((block, 1), lambda i: (i, 0)),
        ],
        out_shape=[
            jax.ShapeDtypeStruct((rows, cols), jnp.bfloat16),
            jax.ShapeDtypeStruct((rows, 1), jnp.float32),
        ],
        cost_estimate=pl.CostEstimate(
            flops=2 * rows * cols * depth, bytes_accessed=2 * rows * cols, transcendentals=rows * cols
        ),
        name="make_kernel",
    )(scores_a, scores_b)


def row_pass(kernel, column_scaling):
    rows, cols = kernel.shape
    block = block_of(rows, 512)
    group = block_of(block, 64)

    def body(k_ref, c_ref, s_ref):
        @pl.loop(0, block // group)
        def _(step):
            base = pl.multiple_of(step * group, group)
            total = jnp.zeros((group, LANES), jnp.float32)
            for lane in range(0, cols, LANES):
                total = total + (
                    k_ref[pl.ds(base, group), lane : lane + LANES].astype(jnp.float32)
                    * c_ref[:, lane : lane + LANES]
                )
            s_ref[pl.ds(base, group), :] = jnp.sum(total, axis=1, keepdims=True)

    return pl.pallas_call(
        body,
        grid=(rows // block,),
        in_specs=[
            pl.BlockSpec((block, cols), lambda i: (i, 0)),
            pl.BlockSpec((1, cols), lambda i: (0, 0)),
        ],
        out_specs=pl.BlockSpec((block, 1), lambda i: (i, 0)),
        out_shape=jax.ShapeDtypeStruct((rows, 1), jnp.float32),
        cost_estimate=pl.CostEstimate(
            flops=2 * rows * cols, bytes_accessed=2 * rows * cols, transcendentals=0
        ),
        name="row_pass",
    )(kernel, column_scaling)


def col_pass(kernel, row_scale):
    rows, cols = kernel.shape
    block = block_of(rows, 512)

    def body(k_ref, r_ref, s_ref):
        @pl.when(pl.program_id(0) == 0)
        def _():
            s_ref[...] = jnp.zeros_like(s_ref)

        for lane in range(0, cols, LANES):
            part = k_ref[:, lane : lane + LANES].astype(jnp.float32) * r_ref[...]
            s_ref[:, lane : lane + LANES] += jnp.sum(part, axis=0, keepdims=True)

    return pl.pallas_call(
        body,
        grid=(rows // block,),
        in_specs=[
            pl.BlockSpec((block, cols), lambda i: (i, 0)),
            pl.BlockSpec((block, LANES), lambda i: (i, 0)),
        ],
        out_specs=pl.BlockSpec((1, cols), lambda i: (0, 0)),
        out_shape=jax.ShapeDtypeStruct((1, cols), jnp.float32),
        cost_estimate=pl.CostEstimate(
            flops=2 * rows * cols, bytes_accessed=2 * rows * cols, transcendentals=0
        ),
        name="col_pass",
    )(kernel, jnp.broadcast_to(row_scale, (rows, LANES)))


def scores_of(gate_pre, up_pre, axis, parts, wire):
    tokens, width = gate_pre.shape
    own = width // parts
    both = jnp.stack((gate_pre.astype(wire), up_pre.astype(wire)))
    both = both.reshape(2, tokens, parts, own).transpose(2, 0, 1, 3)
    summed = lax.psum_scatter(both, axis, scatter_dimension=0, tiled=False).astype(jnp.float32)
    mine = standardize(summed[0], summed[1]).T
    return lax.all_gather(mine, axis, axis=0, tiled=True)


def solution(mesh):
    n_row, n_col = mesh.shape["row"], mesh.shape["col"]

    def per_device(calib, gate_a, up_a, gate_b, up_b, down_a, down_b):
        width_a = gate_a.shape[0]
        width_b = gate_b.shape[0]
        inputs_a = lax.dynamic_slice_in_dim(calib, lax.axis_index("col") * width_a, width_a, 1)
        inputs_b = lax.dynamic_slice_in_dim(calib, lax.axis_index("row") * width_b, width_b, 1)
        gate_pre_a = jnp.dot(inputs_a, gate_a, preferred_element_type=jnp.float32)
        up_pre_a = jnp.dot(inputs_a, up_a, preferred_element_type=jnp.float32)
        gate_pre_b = jnp.dot(inputs_b, gate_b, preferred_element_type=jnp.float32)
        up_pre_b = jnp.dot(inputs_b, up_b, preferred_element_type=jnp.float32)
        scores_a = scores_of(gate_pre_a, up_pre_a, "col", n_col, jnp.bfloat16)
        scores_b = scores_of(gate_pre_b, up_pre_b, "row", n_row, jnp.float32)
        rows_full = lax.all_gather(down_b, "row", axis=1, tiled=True)
        multiplier = 1.0 / (calib.shape[0] * softness)
        kernel, row_part = make_kernel(scores_a, scores_b, multiplier)
        for step in range(ITERS):
            if step:
                row_part = row_pass(kernel, column_scaling)
            row_scale = 1.0 / lax.psum(row_part[:, 0], "col")[:, None]
            column_scaling = 1.0 / lax.psum(col_pass(kernel, row_scale), "row")
        scaled = (rows_full.astype(jnp.float32) * column_scaling.reshape(-1, 1)).astype(jnp.bfloat16)
        window = scaled.shape[1]
        pieces = []
        for cut in range(0, window, window // 4):
            part = jnp.dot(kernel, scaled[:, cut : cut + window // 4], preferred_element_type=jnp.float32)
            part = (part * row_scale).astype(jnp.bfloat16)
            pieces.append(lax.psum_scatter(part, "col", scatter_dimension=0, tiled=True))
        aligned = jnp.concatenate(pieces, axis=1).astype(jnp.float32)
        return ((down_a.astype(jnp.float32) + aligned) * 0.5).astype(jnp.bfloat16)

    placed = (
        P(),
        P("col", "row"),
        P("col", "row"),
        P("row", "col"),
        P("row", "col"),
        P(("row", "col"), None),
        P("col", "row"),
    )
    return jax.shard_map(
        per_device, mesh=mesh, in_specs=placed, out_specs=P(("row", "col"), None), check_vma=False
    )
```
